32 devices in a mesh: fsdp: 32 (over z, y, x, core).
Axes of the slice: x: 2, y: 2, z: 4, core: 2. Of those that a mesh axis runs over, the one named last changes fastest.
Arguments:
- tokens: bfloat16 [4096, 1024], P('fsdp'), may hold values from -6 to 6
- cotangent: bfloat16 [4096, 1024], P('fsdp'), may hold values from -6 to 6
- seq_len: int32 [128], P('fsdp'), may hold values from 0 to 128, as said below
- gain_one: bfloat16 [1024], P('fsdp'), may hold values from 0.5 to 1.5
- w_qkv: bfloat16 [1024, 3072], P('fsdp'), may hold values from -0.1875 to 0.1875
- w_out: bfloat16 [1024, 1024], P('fsdp'), may hold values from -0.5 to 0.5
- gain_two: bfloat16 [1024], P('fsdp'), may hold values from 0.5 to 1.5
- w_in: bfloat16 [1024, 5248], P('fsdp'), may hold values from -0.1875 to 0.1875
- w_down: bfloat16 [1024, 2624], P('fsdp'), may hold values from -0.125 to 0.125
- m_gain_one: float32 [1024], P('fsdp'), may hold values from -40 to 40
- v_gain_one: float32 [1024], P('fsdp'), may hold values from 0.6144 to 6.144
- m_qkv: float32 [1024, 3072], P('fsdp'), may hold values from -40 to 40
- v_qkv: float32 [1024, 3072], P('fsdp'), may hold values from 0.6144 to 6.144
- m_out: float32 [1024, 1024], P('fsdp'), may hold values from -20 to 20
- v_out: float32 [1024, 1024], P('fsdp'), may hold values from 0.16384 to 1.6384
- m_gain_two: float32 [1024], P('fsdp'), may hold values from -40 to 40
- v_gain_two: float32 [1024], P('fsdp'), may hold values from 0.6144 to 6.144
- m_in: float32 [1024, 5248], P('fsdp'), may hold values from -16 to 16
- v_in: float32 [1024, 5248], P('fsdp'), may hold values from 0.11186 to 1.1186
- m_down: float32 [1024, 2624], P('fsdp'), may hold values from -32 to 32
- v_down: float32 [1024, 2624], P('fsdp'), may hold values from 0.32768 to 3.2768
Outputs:
- output: bfloat16 [4096, 1024], P('fsdp')
- grad_tokens: float32 [4096, 1024], P('fsdp')
- grad_gain_one: float32 [1024], P('fsdp')
- grad_qkv: float32 [1024, 3072], P('fsdp')
- grad_out: float32 [1024, 1024], P('fsdp')
- grad_gain_two: float32 [1024], P('fsdp')
- grad_in: float32 [1024, 5248], P('fsdp')
- grad_down: float32 [1024, 2624], P('fsdp')
- new_gain_one: float32 [1024], P('fsdp')
- new_qkv: float32 [1024, 3072], P('fsdp')
- new_out: float32 [1024, 1024], P('fsdp')
- new_gain_two: float32 [1024], P('fsdp')
- new_in: float32 [1024, 5248], P('fsdp')
- new_down: float32 [1024, 2624], P('fsdp')
- new_m_gain_one: float32 [1024], P('fsdp')
- new_v_gain_one: float32 [1024], P('fsdp')
- new_m_qkv: float32 [1024, 3072], P('fsdp')
- new_v_qkv: float32 [1024, 3072], P('fsdp')
- new_m_out: float32 [1024, 1024], P('fsdp')
- new_v_out: float32 [1024, 1024], P('fsdp')
- new_m_gain_two: float32 [1024], P('fsdp')
- new_v_gain_two: float32 [1024], P('fsdp')
- new_m_in: float32 [1024, 5248], P('fsdp')
- new_v_in: float32 [1024, 5248], P('fsdp')
- new_m_down: float32 [1024, 2624], P('fsdp')
- new_v_down: float32 [1024, 2624], P('fsdp')
The draws below stay inside these ranges and needn't reach their ends.
Inputs may be any that keep to these rules, and one draw needn't show every extreme that they name: `seq_len`: A slot of length 0 holds no sequence; the lengths of one device never add up to more than 128; some slot holds a sequence of 128 tokens.
All inputs are finite; a program needn't handle non-finite values.
Results may differ from the reference program's by a relative error of at most 0.014.
Values may be sent and summed in bfloat16 or wider, within the bound.
A program may use at most 256 MiB of HBM per device.

```python
import math
from functools import partial
import jax
import jax.numpy as jnp
from jax import lax

D = 1024
HD = 64
FF = 2624
CAP = 128
L_MAX = 128
SEQ_DEV = 4
STEP = 4
TOKENS = 4096
NSEQ = 128
N_FSDP = 32


def draw_seq_len(key, part):
    devices_here = NSEQ // SEQ_DEV
    key_len, key_pick = jax.random.split(key)
    raw = jax.random.randint(key_len, (devices_here, SEQ_DEV), 1, L_MAX + 1, dtype=jnp.int32)
    chosen = jax.random.randint(key_pick, (), 0, devices_here, dtype=jnp.int32)
    rows_index = jnp.arange(devices_here, dtype=jnp.int32)[:, None]
    slot_index = jnp.arange(SEQ_DEV, dtype=jnp.int32)[None, :]
    forced = (rows_index == chosen) & (slot_index == 0)
    raw = jnp.where(forced, jnp.int32(L_MAX), raw)
    ends = jnp.cumsum(raw, axis=1, dtype=jnp.int32)
    return jnp.where(ends <= CAP, raw, jnp.int32(0)).reshape(-1)


def spiked(array, key, source, target, shards_of, factor):
    owner, partner = [(jnp.arange(array.shape[dim]) // (array.shape[dim] // shards_of)).reshape([-1 if axis == dim else 1 for axis in range(array.ndim)]) for dim in (source, target)]
    chosen = jax.random.permutation(key, shards_of)[partner]
    strong = (owner == chosen) | (owner == (partner + shards_of // 2) % shards_of)
    return jnp.where(strong, factor * array, array)


def levels(rng, dims, shards, smallest, high):
    loudness = 1.0
    for axis_at, blocks in shards:
        steps = jax.random.uniform(jax.random.fold_in(jax.random.fold_in(rng, 6), axis_at), (blocks,), jnp.float32, smallest / len(shards), high / len(shards))
        loudness = loudness * jnp.repeat(jnp.exp(steps), dims[axis_at] // blocks).reshape((-1,) + (1,) * (len(dims) - 1 - axis_at))
    return loudness


def noise(own_key, dims, scale, bound, cuts=(), kind=jnp.bfloat16):
    factor_of = levels(own_key, dims, cuts, -0.22, 0.18) if cuts else 1.0
    array = jax.random.normal(own_key, dims, jnp.float32) * scale * factor_of
    return jnp.minimum(jnp.maximum(array, -bound), bound).astype(kind)


def bell_draw_with(rng, shape, deviation, reach, cuts, heavy, kind=jnp.bfloat16):
    drawn = deviation * jax.random.normal(rng, shape, jnp.float32)
    if cuts:
        drawn = drawn * levels(rng, shape, cuts, -0.22, 0.18)
    return jnp.clip(spiked(drawn, jax.random.fold_in(rng, 3), *heavy), -reach, reach).astype(kind)


def setup_inputs(seed: int = 0) -> dict:
    key_list = jax.random.split(jax.random.key(seed), 22)
    return {
        "tokens": noise(key_list[0], (TOKENS, D), 1.0, 6.0, ((0, 32),)),
        "cotangent": bell_draw_with(key_list[1], (TOKENS, D), 1.0, 6.0, ((0, 32),), (0, 1, 32, 2.75)),
        "seq_len": draw_seq_len(jax.random.fold_in(key_list[21], 71), 0),
        "gain_one": jnp.clip(1.0 + 0.1 * jax.random.normal(key_list[3], (D,), jnp.float32), 0.5, 1.5).astype(jnp.bfloat16),
        "w_qkv": noise(key_list[4], (D, 3 * D), D ** -0.5, 0.1875, ((0, 32),)),
        "w_out": noise(key_list[5], (D, D), (D // 8) ** -0.5, 0.5, ((0, 32),)),
        "gain_two": jnp.clip(1.0 + 0.1 * jax.random.normal(key_list[6], (D,), jnp.float32), 0.5, 1.5).astype(jnp.bfloat16),
        "w_in": noise(key_list[7], (D, 2 * FF), D ** -0.5, 0.1875, ((0, 32),)),
        "w_down": noise(key_list[8], (D, FF), FF ** -0.5, 0.125, ((0, 32),)),
        "m_gain_one": noise(key_list[9], (D,), (0.1 * TOKENS ** 0.5), 40.0, ((0, 32),), jnp.float32),
        "v_gain_one": jnp.clip(jnp.exp(math.log(6.144) - 2.3025851 * jax.random.uniform(key_list[10], (D,), jnp.float32) ** levels(key_list[10], (D,), ((0, 32),), -0.2, 0.2)), 0.6144, 6.144),
        "m_qkv": noise(key_list[11], (D, 3 * D), (0.1 * TOKENS ** 0.5), 40.0, ((0, 32),), jnp.float32),
        "v_qkv": jnp.clip(jnp.exp(math.log(6.144) - 2.3025851 * jax.random.uniform(key_list[12], (D, 3 * D), jnp.float32) ** levels(key_list[12], (D, 3 * D), ((0, 32),), -0.2, 0.2)), 0.6144, 6.144),
        "m_out": noise(key_list[13], (D, D), (0.055 * TOKENS ** 0.5), 20.0, ((0, 32),), jnp.float32),
        "v_out": jnp.clip(jnp.exp(math.log(1.6384) - 2.3025851 * jax.random.uniform(key_list[14], (D, D), jnp.float32) ** levels(key_list[14], (D, D), ((0, 32),), -0.2, 0.2)), 0.16384, 1.6384),
        "m_gain_two": noise(key_list[15], (D,), (0.1 * TOKENS ** 0.5), 40.0, ((0, 32),), jnp.float32),
        "v_gain_two": jnp.clip(jnp.exp(math.log(6.144) - 2.3025851 * jax.random.uniform(key_list[16], (D,), jnp.float32) ** levels(key_list[16], (D,), ((0, 32),), -0.2, 0.2)), 0.6144, 6.144),
        "m_in": noise(key_list[17], (D, 2 * FF), (0.07 * (TOKENS * D // FF) ** 0.5), 16.0, ((0, 32),), jnp.float32),
        "v_in": jnp.clip(jnp.exp(math.log(1.1186) - 2.3025851 * jax.random.uniform(key_list[18], (D, 2 * FF), jnp.float32) ** levels(key_list[18], (D, 2 * FF), ((0, 32),), -0.2, 0.2)), 0.11186, 1.1186),
        "m_down": noise(key_list[19], (D, FF), (0.08 * TOKENS ** 0.5), 32.0, ((0, 32),), jnp.float32),
        "v_down": jnp.clip(jnp.exp(math.log(3.2768) - 2.3025851 * jax.random.uniform(key_list[20], (D, FF), jnp.float32) ** levels(key_list[20], (D, FF), ((0, 32),), -0.2, 0.2)), 0.32768, 3.2768),
    }


eps_norm = 1e-05
eps_adam = 1e-08
rope_base = 160000.0
beta_one = 0.9
beta_two = 0.999
rate_matrix = 0.01
rate_gain = 0.1
decay_matrix = 0.1
score_scale = 0.125
masked_score = -1e+30

def placing(lengths, rows):
    ends = jnp.cumsum(lengths, dtype=jnp.int32)
    starts = ends - lengths
    places = jnp.arange(rows, dtype=jnp.int32)
    inside = ((places[None, :] >= starts[:, None]) & (places[None, :] < ends[:, None])).astype(jnp.int32)
    slots = jnp.arange(lengths.shape[0], dtype=jnp.int32)
    valid = lax.optimization_barrier(jnp.sum(inside, axis=0, dtype=jnp.int32))
    segment = lax.optimization_barrier(jnp.sum(inside * slots[:, None], axis=0, dtype=jnp.int32)) + (1 - valid) * lengths.shape[0]
    position = places - lax.optimization_barrier(jnp.sum(inside * starts[:, None], axis=0, dtype=jnp.int32))
    return (segment, position, valid)

def rope_tables(position):
    exponent = jnp.arange(HD // 2, dtype=jnp.float32) * (-2.0 / HD)
    inverse = jnp.exp(exponent * math.log(rope_base))
    angles = position.astype(jnp.float32)[:, None] * inverse[None, :]
    return (jnp.cos(angles), jnp.sin(angles))

def rotate(tensor, rot_cos, rot_sin):
    half = tensor.shape[-1] // 2
    first = tensor[..., :half]
    second = tensor[..., half:]
    cosine = rot_cos[:, None, :]
    sinus = rot_sin[:, None, :]
    return jnp.concatenate([first * cosine - second * sinus, second * cosine + first * sinus], axis=-1)

def unrotate(tensor, rot_cos, rot_sin):
    half = tensor.shape[-1] // 2
    first = tensor[..., :half]
    second = tensor[..., half:]
    cosine = rot_cos[:, None, :]
    sinus = rot_sin[:, None, :]
    return jnp.concatenate([first * cosine + second * sinus, second * cosine - first * sinus], axis=-1)

def norm_forward(values_in):
    centre = lax.optimization_barrier(jnp.mean(values_in, axis=-1, keepdims=True))
    centred = values_in - centre
    inv_std = lax.rsqrt(lax.optimization_barrier(jnp.mean(centred * centred, axis=-1, keepdims=True)) + eps_norm)
    return (centred * inv_std, inv_std)

def norm_backward(grad_out, normed, inv_std, gain_f):
    scaled = grad_out * gain_f[None, :]
    first_mean = lax.optimization_barrier(jnp.mean(scaled, axis=-1, keepdims=True))
    second_mean = lax.optimization_barrier(jnp.mean(scaled * normed, axis=-1, keepdims=True))
    grad_input = inv_std * (scaled - first_mean - normed * second_mean)
    grad_gain = lax.optimization_barrier(jnp.sum(grad_out * normed, axis=0))
    return (grad_input, grad_gain)

def rows_product(left, right):
    return lax.dot_general(left, right, (((0,), (0,)), ((), ())), preferred_element_type=jnp.float32)

def back_product(left, right):
    return lax.dot_general(left, right, (((1,), (1,)), ((), ())), preferred_element_type=jnp.float32)

def allowed_pairs(segment):
    return (segment[:, None] == segment[None, :])[None, :, :]

def attend_forward(queries, keys, values, segment):
    scores = jnp.einsum('rhd,shd->hrs', queries.astype(jnp.float32), keys.astype(jnp.float32)) * score_scale
    scores = jnp.where(allowed_pairs(segment), scores, masked_score)
    row_max = lax.optimization_barrier(jnp.max(scores, axis=-1, keepdims=True))
    row_sum = lax.optimization_barrier(jnp.sum(jnp.exp(scores - row_max), axis=-1, keepdims=True))
    log_total = row_max + jnp.log(row_sum)
    probs = jnp.exp(scores - log_total).astype(jnp.bfloat16)
    attended = jnp.einsum('hrs,shd->rhd', probs.astype(jnp.float32), values.astype(jnp.float32))
    return (attended.astype(jnp.bfloat16), log_total)

def attend_backward(queries, keys, values, segment, attended, log_total, grad_att):
    scores = jnp.einsum('rhd,shd->hrs', queries.astype(jnp.float32), keys.astype(jnp.float32)) * score_scale
    scores = jnp.where(allowed_pairs(segment), scores, masked_score)
    probs = jnp.exp(scores - log_total)
    probs_b = probs.astype(jnp.bfloat16)
    grad_values = jnp.einsum('hrs,rhd->shd', probs_b.astype(jnp.float32), grad_att.astype(jnp.float32))
    grad_probs = jnp.einsum('rhd,shd->hrs', grad_att.astype(jnp.float32), values.astype(jnp.float32))
    delta = jnp.transpose(lax.optimization_barrier(jnp.sum(grad_att.astype(jnp.float32) * attended.astype(jnp.float32), axis=-1)))[:, :, None]
    grad_scores = (probs * (grad_probs - delta) * score_scale).astype(jnp.bfloat16)
    grad_queries = jnp.einsum('hrs,shd->rhd', grad_scores.astype(jnp.float32), keys.astype(jnp.float32))
    grad_keys = jnp.einsum('hrs,rhd->shd', grad_scores.astype(jnp.float32), queries.astype(jnp.float32))
    return (grad_queries, grad_keys, grad_values)

def forward_pass(tokens, lengths, weights):
    gain_one, w_qkv, w_out, gain_two, w_in, w_down = weights
    groups = lengths.shape[0]
    rows = tokens.shape[0]
    per_dev = rows // groups
    width = tokens.shape[1]
    heads = width // HD
    ffw = w_in.shape[1] // 2
    segment, position, valid = jax.vmap(partial(placing, rows=per_dev))(lengths)
    rot_cos, rot_sin = rope_tables(position.reshape(rows))
    base = tokens.astype(jnp.float32)
    normed_one, inv_one = norm_forward(base)
    hidden_one = (normed_one * gain_one.astype(jnp.float32)[None, :]).astype(jnp.bfloat16)
    projected = jnp.dot(hidden_one, w_qkv, preferred_element_type=jnp.float32).reshape(rows, 3, heads, HD)
    queries = rotate(projected[:, 0], rot_cos, rot_sin).astype(jnp.bfloat16)
    keys = rotate(projected[:, 1], rot_cos, rot_sin).astype(jnp.bfloat16)
    values = projected[:, 2].astype(jnp.bfloat16)
    shape_four = (groups, per_dev, heads, HD)
    attended, log_total = jax.vmap(attend_forward)(queries.reshape(shape_four), keys.reshape(shape_four), values.reshape(shape_four), segment)
    attended_flat = attended.reshape(rows, width)
    residual = base + jnp.dot(attended_flat, w_out, preferred_element_type=jnp.float32)
    normed_two, inv_two = norm_forward(residual)
    hidden_two = (normed_two * gain_two.astype(jnp.float32)[None, :]).astype(jnp.bfloat16)
    lifted = jnp.dot(hidden_two, w_in, preferred_element_type=jnp.float32)
    inner = lifted[:, :ffw]
    gate_part = lifted[:, ffw:]
    cdf = 0.5 * (1.0 + jax.scipy.special.erf(inner * (1.0 / math.sqrt(2.0))))
    activated = inner * cdf
    mixed = (activated * gate_part).astype(jnp.bfloat16)
    output = (residual + back_product(mixed, w_down)).astype(jnp.bfloat16)
    saved = {'valid': valid.reshape(rows), 'segment': segment, 'rot_cos': rot_cos, 'rot_sin': rot_sin, 'normed_one': normed_one, 'inv_one': inv_one, 'hidden_one': hidden_one, 'queries': queries.reshape(shape_four), 'keys': keys.reshape(shape_four), 'values': values.reshape(shape_four), 'attended': attended, 'log_total': log_total, 'attended_flat': attended_flat, 'normed_two': normed_two, 'inv_two': inv_two, 'hidden_two': hidden_two, 'inner': inner, 'gate_part': gate_part, 'cdf': cdf, 'activated': activated, 'mixed': mixed}
    return (output, saved)

def backward_mlp(cotangent, saved, weights):
    gain_one, w_qkv, w_out, gain_two, w_in, w_down = weights
    grad_rows = cotangent.astype(jnp.float32) * saved['valid'].astype(jnp.float32)[:, None]
    grad_rows_b = grad_rows.astype(jnp.bfloat16)
    grad_down = rows_product(grad_rows_b, saved['mixed'])
    grad_mixed = jnp.dot(grad_rows_b, w_down, preferred_element_type=jnp.float32)
    inner = saved['inner']
    density = jnp.exp(-0.5 * inner * inner) * (1.0 / math.sqrt(2.0 * math.pi))
    grad_inner = grad_mixed * saved['gate_part'] * (saved['cdf'] + inner * density)
    grad_gate = grad_mixed * saved['activated']
    grad_lift = jnp.concatenate([grad_inner, grad_gate], axis=1).astype(jnp.bfloat16)
    grad_in = rows_product(saved['hidden_two'], grad_lift)
    grad_hidden_two = back_product(grad_lift, w_in)
    grad_norm_two, grad_gain_two = norm_backward(grad_hidden_two, saved['normed_two'], saved['inv_two'], gain_two.astype(jnp.float32))
    grad_resid = grad_rows + grad_norm_two
    return (grad_resid, (grad_gain_two, grad_in, grad_down))

def backward_attention(grad_resid, saved, weights):
    gain_one, w_qkv, w_out, gain_two, w_in, w_down = weights
    shape_four = saved['queries'].shape
    rows = grad_resid.shape[0]
    width = grad_resid.shape[1]
    grad_resid_b = grad_resid.astype(jnp.bfloat16)
    grad_wout = rows_product(saved['attended_flat'], grad_resid_b)
    grad_att = back_product(grad_resid_b, w_out).astype(jnp.bfloat16).reshape(shape_four)
    grad_queries, grad_keys, grad_values = jax.vmap(attend_backward)(saved['queries'], saved['keys'], saved['values'], saved['segment'], saved['attended'], saved['log_total'], grad_att)
    three_shape = (rows, shape_four[2], shape_four[3])
    grad_queries = unrotate(grad_queries.reshape(three_shape), saved['rot_cos'], saved['rot_sin'])
    grad_keys = unrotate(grad_keys.reshape(three_shape), saved['rot_cos'], saved['rot_sin'])
    grad_values = grad_values.reshape(three_shape)
    grad_proj = jnp.stack([grad_queries, grad_keys, grad_values], axis=1).reshape(rows, 3 * width).astype(jnp.bfloat16)
    grad_qkv = rows_product(saved['hidden_one'], grad_proj)
    grad_hidden_one = back_product(grad_proj, w_qkv)
    grad_norm_one, grad_gain_one = norm_backward(grad_hidden_one, saved['normed_one'], saved['inv_one'], gain_one.astype(jnp.float32))
    grad_tokens = grad_resid + grad_norm_one
    return (grad_tokens, (grad_gain_one, grad_qkv, grad_wout))

def adamw(weight, gradient, first, second, count, rate, decay):
    first_new = beta_one * first + (1.0 - beta_one) * gradient
    second_new = beta_two * second + (1.0 - beta_two) * gradient * gradient
    correct_one = 1.0 - jnp.power(beta_one, count)
    correct_two = 1.0 - jnp.power(beta_two, count)
    weight_f = weight.astype(jnp.float32)
    update = first_new / correct_one / (jnp.sqrt(second_new / correct_two) + eps_adam) + decay * weight_f
    return (weight_f - rate * update, first_new, second_new)

def reference(tokens, cotangent, seq_len, gain_one, w_qkv, w_out, gain_two, w_in, w_down, m_gain_one, v_gain_one, m_qkv, v_qkv, m_out, v_out, m_gain_two, v_gain_two, m_in, v_in, m_down, v_down):
    group = 16 if N_FSDP % 16 == 0 else 1
    blocks = N_FSDP // group
    rows = group * CAP
    weights = (gain_one, w_qkv, w_out, gain_two, w_in, w_down)
    tok_blocks = tokens.reshape(blocks, rows, D)
    cot_blocks = cotangent.reshape(blocks, rows, D)
    len_blocks = seq_len.reshape(blocks, group, SEQ_DEV)
    zeros = tuple((jnp.zeros(weight.shape, jnp.float32) for weight in weights))

    def visit(carry, block):
        tok_rows, cot_rows, lens = block
        output, saved = forward_pass(tok_rows, lens, weights)
        grad_resid, mlp_grads = backward_mlp(cot_rows, saved, weights)
        grad_rows_in, att_grads = backward_attention(grad_resid, saved, weights)
        grads = (att_grads[0], att_grads[1], att_grads[2], mlp_grads[0], mlp_grads[1], mlp_grads[2])
        carry = tuple((left + right for left, right in zip(carry, grads)))
        return (carry, (output, grad_rows_in))
    totals, (outputs, grad_rows_all) = lax.scan(visit, zeros, (tok_blocks, cot_blocks, len_blocks))
    count = jnp.asarray(STEP, jnp.float32)
    firsts = (m_gain_one, m_qkv, m_out, m_gain_two, m_in, m_down)
    seconds = (v_gain_one, v_qkv, v_out, v_gain_two, v_in, v_down)
    rates = (rate_gain, rate_matrix, rate_matrix, rate_gain, rate_matrix, rate_matrix)
    decays = (0.0, decay_matrix, decay_matrix, 0.0, decay_matrix, decay_matrix)
    results = [adamw(weights[i], totals[i], firsts[i], seconds[i], count, rates[i], decays[i]) for i in range(6)]
    return (outputs.reshape(TOKENS, D), grad_rows_all.reshape(TOKENS, D), totals[0], totals[1], totals[2], totals[3], totals[4], totals[5], results[0][0], results[1][0], results[2][0], results[3][0], results[4][0], results[5][0], results[0][1], results[0][2], results[1][1], results[1][2], results[2][1], results[2][2], results[3][1], results[3][2], results[4][1], results[4][2], results[5][1], results[5][2])
```

```python
from functools import partial
import math

import jax
import jax.numpy as jnp
from jax import lax
from jax.sharding import PartitionSpec as P

HD = 64
STEP = 4


eps_norm = 1e-05
eps_adam = 1e-08
rope_base = 160000.0
beta_one = 0.9
beta_two = 0.999
rate_matrix = 0.01
rate_gain = 0.1
decay_matrix = 0.1
score_scale = 0.125
masked_score = -1e30


def swaps(count, bit):
    return [(i, i ^ (1 << bit)) for i in range(count)]


def bit_order(count, stream):
    bits = count.bit_length() - 1
    rest = list(range(bits - 2, 0, -1))
    turn = stream % max(len(rest), 1)
    rest = rest[len(rest) - turn :] + rest[: len(rest) - turn]
    return [bits - 1] + rest + [0]


def gather_rows(shard, count, stream):
    bits = count.bit_length() - 1
    held = shard.reshape((1,) * bits + shard.shape)
    for bit in bit_order(count, stream):
        other = lax.ppermute(held, "fsdp", swaps(count, bit))
        held = jnp.concatenate([held, other], axis=bits - 1 - bit)
    return held.reshape((count * shard.shape[0],) + shard.shape[1:])


def scatter_rows(full, count, stream):
    bits = count.bit_length() - 1
    rows = full.shape[0] // count
    held = full.astype(jnp.bfloat16).reshape((2,) * bits + (rows,) + full.shape[1:])
    order = bit_order(count, stream)[::-1]
    for step, bit in enumerate(order):
        axis = bits - 1 - bit
        kept = lax.slice_in_dim(held, 0, 1, axis=axis)
        sent = lax.slice_in_dim(held, 1, 2, axis=axis)
        other = lax.ppermute(sent, "fsdp", swaps(count, bit))
        held = kept.astype(jnp.float32) + other.astype(jnp.float32)
        if step < len(order) - 1:
            held = held.astype(jnp.bfloat16)
    return held.reshape((rows,) + full.shape[1:])


def sum_small(value, count):
    for bit in range(count.bit_length() - 1):
        value = value + lax.ppermute(value, "fsdp", swaps(count, bit))
    return value


def order_matrix(width, count):
    per = width // count
    me = lax.axis_index("fsdp").astype(jnp.int32)
    spot = jnp.arange(width, dtype=jnp.int32)
    target = jnp.bitwise_xor(spot // per, me) * per + spot % per
    return (target[:, None] == spot[None, :]).astype(jnp.bfloat16)


def reorder(array, order):
    if array.dtype == jnp.bfloat16:
        return jnp.dot(array, order, preferred_element_type=jnp.float32).astype(jnp.bfloat16)
    return jnp.dot(
        array,
        order.astype(jnp.float32),
        precision=lax.Precision.HIGHEST,
        preferred_element_type=jnp.float32,
    )


def placing(lengths, rows):
    ends = jnp.cumsum(lengths, dtype=jnp.int32)
    starts = ends - lengths
    places = jnp.arange(rows, dtype=jnp.int32)
    inside = ((places[None, :] >= starts[:, None]) & (places[None, :] < ends[:, None])).astype(
        jnp.int32
    )
    slots = jnp.arange(lengths.shape[0], dtype=jnp.int32)
    valid = jnp.sum(inside, axis=0, dtype=jnp.int32)
    segment = (
        jnp.sum(inside * slots[:, None], axis=0, dtype=jnp.int32) + (1 - valid) * lengths.shape[0]
    )
    position = places - jnp.sum(inside * starts[:, None], axis=0, dtype=jnp.int32)
    return (segment, position, valid)


def rope_tables(position):
    exponent = jnp.arange(HD // 2, dtype=jnp.float32) * (-2.0 / HD)
    inverse = jnp.exp(exponent * math.log(rope_base))
    angles = position.astype(jnp.float32)[:, None] * inverse[None, :]
    return (jnp.cos(angles), jnp.sin(angles))


def rotate(tensor, rot_cos, rot_sin):
    half = tensor.shape[-1] // 2
    first = tensor[..., :half]
    second = tensor[..., half:]
    cosine = rot_cos[:, None, :]
    sinus = rot_sin[:, None, :]
    return jnp.concatenate(
        [first * cosine - second * sinus, second * cosine + first * sinus], axis=-1
    )


def unrotate(tensor, rot_cos, rot_sin):
    half = tensor.shape[-1] // 2
    first = tensor[..., :half]
    second = tensor[..., half:]
    cosine = rot_cos[:, None, :]
    sinus = rot_sin[:, None, :]
    return jnp.concatenate(
        [first * cosine + second * sinus, second * cosine - first * sinus], axis=-1
    )


def norm_forward(values_in):
    centre = jnp.mean(values_in, axis=-1, keepdims=True)
    centred = values_in - centre
    inv_std = lax.rsqrt(jnp.mean(centred * centred, axis=-1, keepdims=True) + eps_norm)
    return (centred * inv_std, inv_std)


def norm_input_grad(grad_out, normed, inv_std, gain_f):
    scaled = grad_out * gain_f[None, :]
    first_mean = jnp.mean(scaled, axis=-1, keepdims=True)
    second_mean = jnp.mean(scaled * normed, axis=-1, keepdims=True)
    return inv_std * (scaled - first_mean - normed * second_mean)


def rows_product(left, right):
    return lax.dot_general(
        left, right, (((0,), (0,)), ((), ())), preferred_element_type=jnp.float32
    )


def back_product(left, right):
    return lax.dot_general(
        left, right, (((1,), (1,)), ((), ())), preferred_element_type=jnp.float32
    )


def allowed_pairs(segment):
    return (segment[:, None] == segment[None, :])[None, :, :]


def attend_forward(queries, keys, values, segment):
    scores = (
        jnp.einsum("rhd,shd->hrs", queries, keys, preferred_element_type=jnp.float32) * score_scale
    )
    scores = jnp.where(allowed_pairs(segment), scores, masked_score)
    row_max = jnp.max(scores, axis=-1, keepdims=True)
    row_sum = jnp.sum(jnp.exp(scores - row_max), axis=-1, keepdims=True)
    log_total = row_max + jnp.log(row_sum)
    probs = jnp.exp(scores - log_total).astype(jnp.bfloat16)
    attended = jnp.einsum("hrs,shd->rhd", probs, values, preferred_element_type=jnp.float32)
    return (attended.astype(jnp.bfloat16), log_total)


def attend_backward(queries, keys, values, segment, attended, log_total, grad_att):
    scores = (
        jnp.einsum("rhd,shd->hrs", queries, keys, preferred_element_type=jnp.float32) * score_scale
    )
    scores = jnp.where(allowed_pairs(segment), scores, masked_score)
    probs = jnp.exp(scores - log_total)
    probs_b = probs.astype(jnp.bfloat16)
    grad_values = jnp.einsum("hrs,rhd->shd", probs_b, grad_att, preferred_element_type=jnp.float32)
    grad_probs = jnp.einsum("rhd,shd->hrs", grad_att, values, preferred_element_type=jnp.float32)
    delta = jnp.transpose(
        jnp.sum(grad_att.astype(jnp.float32) * attended.astype(jnp.float32), axis=-1)
    )[:, :, None]
    grad_scores = (probs * (grad_probs - delta) * score_scale).astype(jnp.bfloat16)
    grad_queries = jnp.einsum("hrs,shd->rhd", grad_scores, keys, preferred_element_type=jnp.float32)
    grad_keys = jnp.einsum("hrs,rhd->shd", grad_scores, queries, preferred_element_type=jnp.float32)
    return (grad_queries, grad_keys, grad_values)


def forward_pass(tokens, lengths, weights, order):
    gain_one, w_three, w_out, gain_two, w_inner, w_gate, w_down = weights
    groups = lengths.shape[0]
    rows = tokens.shape[0]
    per_dev = rows // groups
    width = tokens.shape[1]
    heads = width // HD
    segment, position, valid = jax.vmap(partial(placing, rows=per_dev))(lengths)
    rot_cos, rot_sin = rope_tables(position.reshape(rows))
    base = tokens.astype(jnp.float32)
    normed_one, inv_one = norm_forward(base)
    hidden_one = (normed_one * gain_one.astype(jnp.float32)[None, :]).astype(jnp.bfloat16)
    hidden_one = reorder(hidden_one, order)
    projected = [
        jnp.dot(hidden_one, part, preferred_element_type=jnp.float32).reshape(rows, heads, HD)
        for part in w_three
    ]
    queries = rotate(projected[0], rot_cos, rot_sin).astype(jnp.bfloat16)
    keys = rotate(projected[1], rot_cos, rot_sin).astype(jnp.bfloat16)
    values = projected[2].astype(jnp.bfloat16)
    shape_four = (groups, per_dev, heads, HD)
    attended, log_total = jax.vmap(attend_forward)(
        queries.reshape(shape_four), keys.reshape(shape_four), values.reshape(shape_four), segment
    )
    attended_flat = reorder(attended.reshape(rows, width), order)
    residual = base + jnp.dot(attended_flat, w_out, preferred_element_type=jnp.float32)
    normed_two, inv_two = norm_forward(residual)
    hidden_two = (normed_two * gain_two.astype(jnp.float32)[None, :]).astype(jnp.bfloat16)
    hidden_two = reorder(hidden_two, order)
    inner = jnp.dot(hidden_two, w_inner, preferred_element_type=jnp.float32)
    gate_part = jnp.dot(hidden_two, w_gate, preferred_element_type=jnp.float32)
    cdf = 0.5 * (1.0 + jax.scipy.special.erf(inner * (1.0 / math.sqrt(2.0))))
    activated = inner * cdf
    mixed = (activated * gate_part).astype(jnp.bfloat16)
    output = (residual + reorder(back_product(mixed, w_down), order)).astype(jnp.bfloat16)
    saved = {
        "valid": valid.reshape(rows),
        "segment": segment,
        "rot_cos": rot_cos,
        "rot_sin": rot_sin,
        "normed_one": normed_one,
        "inv_one": inv_one,
        "hidden_one": hidden_one,
        "queries": queries.reshape(shape_four),
        "keys": keys.reshape(shape_four),
        "values": values.reshape(shape_four),
        "attended": attended,
        "log_total": log_total,
        "attended_flat": attended_flat,
        "normed_two": normed_two,
        "inv_two": inv_two,
        "hidden_two": hidden_two,
        "inner": inner,
        "gate_part": gate_part,
        "cdf": cdf,
        "activated": activated,
        "mixed": mixed,
    }
    return (output, saved)


def backward_mlp(cotangent, saved, weights, order):
    gain_one, w_three, w_out, gain_two, w_inner, w_gate, w_down = weights
    grad_rows = cotangent.astype(jnp.float32) * saved["valid"].astype(jnp.float32)[:, None]
    grad_rows_b = reorder(grad_rows.astype(jnp.bfloat16), order)
    grad_mixed = jnp.dot(grad_rows_b, w_down, preferred_element_type=jnp.float32)
    inner = saved["inner"]
    density = jnp.exp(-0.5 * inner * inner) * (1.0 / math.sqrt(2.0 * math.pi))
    grad_inner = grad_mixed * saved["gate_part"] * (saved["cdf"] + inner * density)
    grad_inner = grad_inner.astype(jnp.bfloat16)
    grad_gate = (grad_mixed * saved["activated"]).astype(jnp.bfloat16)
    grad_hidden_two = reorder(
        back_product(grad_inner, w_inner) + back_product(grad_gate, w_gate), order
    )
    grad_norm_two = norm_input_grad(
        grad_hidden_two, saved["normed_two"], saved["inv_two"], gain_two.astype(jnp.float32)
    )
    grad_resid = grad_rows + grad_norm_two
    return (grad_resid, (grad_rows_b, grad_inner, grad_gate, grad_hidden_two))


def backward_attention(grad_resid, saved, weights, order):
    gain_one, w_three, w_out, gain_two, w_inner, w_gate, w_down = weights
    shape_four = saved["queries"].shape
    rows = grad_resid.shape[0]
    width = grad_resid.shape[1]
    grad_resid_b = grad_resid.astype(jnp.bfloat16)
    grad_att = reorder(
        back_product(grad_resid_b, w_out).astype(jnp.bfloat16), order
    ).reshape(shape_four)
    grad_queries, grad_keys, grad_values = jax.vmap(attend_backward)(
        saved["queries"],
        saved["keys"],
        saved["values"],
        saved["segment"],
        saved["attended"],
        saved["log_total"],
        grad_att,
    )
    three_shape = (rows, shape_four[2], shape_four[3])
    grad_queries = unrotate(grad_queries.reshape(three_shape), saved["rot_cos"], saved["rot_sin"])
    grad_keys = unrotate(grad_keys.reshape(three_shape), saved["rot_cos"], saved["rot_sin"])
    grad_proj = [
        part.reshape(rows, width).astype(jnp.bfloat16)
        for part in (grad_queries, grad_keys, grad_values)
    ]
    grad_hidden_one = reorder(
        back_product(grad_proj[0], w_three[0])
        + back_product(grad_proj[1], w_three[1])
        + back_product(grad_proj[2], w_three[2]),
        order,
    )
    grad_norm_one = norm_input_grad(
        grad_hidden_one, saved["normed_one"], saved["inv_one"], gain_one.astype(jnp.float32)
    )
    grad_tokens = grad_resid + grad_norm_one
    return (grad_tokens, (grad_resid_b, grad_proj, grad_hidden_one))


def attention_terms(saved, factors, count):
    grad_resid_b, grad_proj, grad_hidden_one = factors
    sum_out = scatter_rows(rows_product(saved["attended_flat"], grad_resid_b), count, 0)
    sum_three = [
        scatter_rows(rows_product(saved["hidden_one"], part), count, stream)
        for stream, part in enumerate(grad_proj)
    ]
    part_one = jnp.sum(grad_hidden_one * saved["normed_one"], axis=0)
    return (part_one, jnp.concatenate(sum_three, axis=1), sum_out)


def mlp_terms(saved, factors, count):
    grad_rows_b, grad_inner, grad_gate, grad_hidden_two = factors
    sum_down = scatter_rows(rows_product(grad_rows_b, saved["mixed"]), count, 2)
    sum_inner = scatter_rows(rows_product(saved["hidden_two"], grad_inner), count, 0)
    sum_gate = scatter_rows(rows_product(saved["hidden_two"], grad_gate), count, 1)
    part_two = jnp.sum(grad_hidden_two * saved["normed_two"], axis=0)
    return (part_two, jnp.concatenate([sum_inner, sum_gate], axis=1), sum_down)


def own_rows(vector, count):
    per = vector.shape[0] // count
    return lax.dynamic_slice_in_dim(vector, lax.axis_index("fsdp") * per, per)


def adamw(weight, gradient, first, second, count, rate, decay):
    first_new = beta_one * first + (1.0 - beta_one) * gradient
    second_new = beta_two * second + (1.0 - beta_two) * gradient * gradient
    correct_one = 1.0 - jnp.power(beta_one, count)
    correct_two = 1.0 - jnp.power(beta_two, count)
    weight_f = weight.astype(jnp.float32)
    update = (
        first_new / correct_one / (jnp.sqrt(second_new / correct_two) + eps_adam) + decay * weight_f
    )
    return (weight_f - rate * update, first_new, second_new)


def local(
    tokens,
    cotangent,
    seq_len,
    gain_one,
    w_qkv,
    w_out,
    gain_two,
    w_in,
    w_down,
    m_gain_one,
    v_gain_one,
    m_qkv,
    v_qkv,
    m_out,
    v_out,
    m_gain_two,
    v_gain_two,
    m_in,
    v_in,
    m_down,
    v_down,
):
    devices = lax.axis_size("fsdp")
    width = tokens.shape[1]
    ffw = w_down.shape[1]
    order = order_matrix(width, devices)
    gains = gather_rows(jnp.stack([gain_one, gain_two])[None], devices, 0)
    gains = reorder(jnp.transpose(gains, (1, 0, 2)).reshape(2, width), order)
    gathered = (
        gains[0],
        [
            gather_rows(w_qkv[:, i * width : (i + 1) * width], devices, i)
            for i in range(3)
        ],
        gather_rows(w_out, devices, 0),
        gains[1],
        gather_rows(w_in[:, :ffw], devices, 1),
        gather_rows(w_in[:, ffw:], devices, 2),
        gather_rows(w_down, devices, 0),
    )
    output, saved = forward_pass(tokens, seq_len.reshape(1, -1), gathered, order)
    grad_resid, mlp_factors = backward_mlp(cotangent, saved, gathered, order)
    part_two, sum_in, sum_down = mlp_terms(saved, mlp_factors, devices)
    sum_two = own_rows(sum_small(part_two, devices), devices)
    grad_tokens, att_factors = backward_attention(grad_resid, saved, gathered, order)
    part_one, sum_qkv, sum_out = attention_terms(saved, att_factors, devices)
    sum_one = own_rows(sum_small(part_one, devices), devices)
    shards = (sum_one, sum_qkv, sum_out, sum_two, sum_in, sum_down)
    count = jnp.asarray(STEP, jnp.float32)
    weights = (gain_one, w_qkv, w_out, gain_two, w_in, w_down)
    firsts = (m_gain_one, m_qkv, m_out, m_gain_two, m_in, m_down)
    seconds = (v_gain_one, v_qkv, v_out, v_gain_two, v_in, v_down)
    rates = (rate_gain, rate_matrix, rate_matrix, rate_gain, rate_matrix, rate_matrix)
    decays = (0.0, decay_matrix, decay_matrix, 0.0, decay_matrix, decay_matrix)
    results = [
        adamw(weights[i], shards[i], firsts[i], seconds[i], count, rates[i], decays[i])
        for i in range(6)
    ]
    return (
        output,
        grad_tokens,
        shards[0],
        shards[1],
        shards[2],
        shards[3],
        shards[4],
        shards[5],
        results[0][0],
        results[1][0],
        results[2][0],
        results[3][0],
        results[4][0],
        results[5][0],
        results[0][1],
        results[0][2],
        results[1][1],
        results[1][2],
        results[2][1],
        results[2][2],
        results[3][1],
        results[3][2],
        results[4][1],
        results[4][2],
        results[5][1],
        results[5][2],
    )


def solution(mesh):
    placed = (
        P("fsdp", None),
        P("fsdp", None),
        P("fsdp"),
        P("fsdp"),
        P("fsdp", None),
        P("fsdp", None),
        P("fsdp"),
        P("fsdp", None),
        P("fsdp", None),
        P("fsdp"),
        P("fsdp"),
        P("fsdp", None),
        P("fsdp", None),
        P("fsdp", None),
        P("fsdp", None),
        P("fsdp"),
        P("fsdp"),
        P("fsdp", None),
        P("fsdp", None),
        P("fsdp", None),
        P("fsdp", None),
    )
    return jax.shard_map(
        local,
        mesh=mesh,
        in_specs=placed,
        out_specs=(
            P("fsdp", None),
            P("fsdp", None),
            P("fsdp"),
            P("fsdp", None),
            P("fsdp", None),
            P("fsdp"),
            P("fsdp", None),
            P("fsdp", None),
            P("fsdp"),
            P("fsdp", None),
            P("fsdp", None),
            P("fsdp"),
            P("fsdp", None),
            P("fsdp", None),
            P("fsdp"),
            P("fsdp"),
            P("fsdp", None),
            P("fsdp", None),
            P("fsdp", None),
            P("fsdp", None),
            P("fsdp"),
            P("fsdp"),
            P("fsdp", None),
            P("fsdp", None),
            P("fsdp", None),
            P("fsdp", None),
        ),
        check_vma=False,
    )
```
